768 devices in a mesh: chan: 96 (over z, x, core), kred: 8 (over y).
Axes of the slice: x: 4, y: 8, z: 12, core: 2. Of those that a mesh axis runs over, the one named last changes fastest.
Arguments:
- t2_ph: bfloat16 [96, 4096, 128], P('chan', 'kred'), may hold values from -6 to 6
- dest_owner: int32 [96, 4096], P('chan', 'kred'), may hold values from 0 to 95, as said below
- source_owner: int32 [96, 4096], P('chan', 'kred'), may hold values from 0 to 95, as said below
- source_slot: int32 [96, 4096], P('chan', 'kred'), may hold values from 0 to 9
- hole_count: int32 [96], P('chan'), may hold values from 32 to 128
- ladder_v: bfloat16 [96, 4096, 4096], P('chan', None, 'kred'), as said below
Outputs:
- ladder_out: bfloat16 [96, 4096, 128], P('chan', 'kred')
The draws below stay inside these ranges and needn't reach their ends.
Inputs may be any that keep to these rules, and one draw needn't show every extreme that they name: Within each aligned block of 512 rows of dest_owner[s] at most 10 rows name the same channel, and some channel is named by exactly 10; every channel is named by exactly 512 rows of the same block index over all s. The pairs (source_owner, source_slot) of one channel and one aligned block of 512 columns are distinct and name exactly the rows that dest_owner sends to that channel from that block. `ladder_v`: symmetric in its last two dimensions for each channel.
All inputs are finite; a program needn't handle non-finite values.
Results may differ from the reference program's by a relative error of at most 0.001.
Values may be sent and summed in bfloat16 or wider, within the bound.
No kernel may reach another device: no remote copies, remote signals or barrier semaphores. Data moves between devices by JAX's collectives and lax.ppermute only.
A program may use at most 32 MiB of HBM per device.

```python
import jax
import jax.numpy as jnp
from jax import lax

P_SIZE = 4096
H = 128
SLAB = 512
RECV_CAP = 10
N_CHAN = 96
N_KRED = 8


def recouple_lists(key):
    seeded = jax.random.fold_in(key, 7)
    keys = jax.random.split(seeded, 4)
    base_rows = SLAB // N_CHAN
    extra_rows = SLAB % N_CHAN
    channels = jnp.arange(N_CHAN, dtype=jnp.int32)
    base_weights = base_rows + (channels >= N_CHAN - extra_rows).astype(jnp.int32)
    busiest_offset = 0 if RECV_CAP == 2 * base_rows else N_CHAN - 1
    emptied_offset = 1 if busiest_offset == 0 else 0
    base_weights = base_weights + base_rows * (channels == busiest_offset).astype(jnp.int32) - base_rows * (channels == emptied_offset).astype(jnp.int32)
    shifts = jax.random.randint(keys[0], (N_KRED,), 0, N_CHAN)
    weights = base_weights[(channels[None, :] + shifts[:, None]) % N_CHAN]
    offsets = (channels[None, :] - channels[:, None]) % N_CHAN
    counts = weights[:, offsets]
    positions = jnp.arange(SLAB, dtype=jnp.int32)
    cumulative = jnp.cumsum(counts, axis=2)
    sorted_dest = jnp.sum((cumulative[:, :, None, :] <= positions[None, None, :, None]).astype(jnp.int32), axis=3)
    send_keys = jax.random.split(keys[2], N_KRED * N_CHAN)
    send_perms = jax.vmap(lambda kk: jax.random.permutation(kk, SLAB).astype(jnp.int32))(send_keys).reshape(N_KRED, N_CHAN, SLAB)
    dest = jnp.take_along_axis(sorted_dest, send_perms, axis=2)
    dest_owner = jnp.transpose(dest, (1, 0, 2)).reshape(N_CHAN, N_KRED * SLAB)
    incoming = jnp.transpose(counts, (0, 2, 1))
    cum_in = jnp.cumsum(incoming, axis=2)
    src_sorted = jnp.sum((cum_in[:, :, None, :] <= positions[None, None, :, None]).astype(jnp.int32), axis=3)
    starts = jnp.take_along_axis(cum_in - incoming, src_sorted, axis=2)
    slot_sorted = positions[None, None, :] - starts
    recv_keys = jax.random.split(keys[3], N_KRED * N_CHAN)
    recv_perms = jax.vmap(lambda kk: jax.random.permutation(kk, SLAB).astype(jnp.int32))(recv_keys).reshape(N_KRED, N_CHAN, SLAB)
    inverse = jnp.argsort(recv_perms, axis=2).astype(jnp.int32)
    src_owner = jnp.take_along_axis(src_sorted, inverse, axis=2)
    src_slot = jnp.take_along_axis(slot_sorted, inverse, axis=2)
    src_owner = jnp.transpose(src_owner, (1, 0, 2)).reshape(N_CHAN, N_KRED * SLAB)
    src_slot = jnp.transpose(src_slot, (1, 0, 2)).reshape(N_CHAN, N_KRED * SLAB)
    return (dest_owner.astype(jnp.int32), src_owner.astype(jnp.int32), src_slot.astype(jnp.int32))


def draw_dest_owner(key, part):
    return recouple_lists(key)[0]


def draw_source_owner(key, part):
    return recouple_lists(key)[1]


def draw_source_slot(key, part):
    return recouple_lists(key)[2]


def draw_hole_count(key, part):
    seeded = jax.random.fold_in(key, 11)
    first, second = jax.random.split(seeded)
    counts = jax.random.randint(first, (N_CHAN,), H // 4, H + 1).astype(jnp.int32)
    fullest = jax.random.randint(second, (), 0, N_CHAN)
    return counts.at[fullest].set(H)


def draw_ladder_v(key, part):
    seeded = jax.random.fold_in(key, 13)
    raw = jax.random.normal(seeded, (N_CHAN, P_SIZE, P_SIZE), jnp.float32)
    symmetric = (raw + jnp.swapaxes(raw, 1, 2)) * (1.0 / (2.0 * P_SIZE) ** 0.5)
    return symmetric.astype(jnp.bfloat16)


def shard_levels(key, dims, pieces, low, high):
    gain, own = 1.0, jax.random.fold_in(key, 6)
    for axis_at, parts in pieces:
        steps = jnp.exp(jax.random.uniform(jax.random.fold_in(own, axis_at), (parts,), jnp.float32, low / len(pieces), high / len(pieces)))
        gain = gain * jnp.repeat(steps, dims[axis_at] // parts).reshape([-1 if axis == axis_at else 1 for axis in range(len(dims))])
    return gain


def normal_values(stream_key, extent, width, reach, cuts=(), held_as=jnp.bfloat16):
    drawn = width * jax.random.normal(stream_key, extent, jnp.float32)
    if cuts:
        drawn = drawn * shard_levels(stream_key, extent, cuts, -0.22, 0.18)
    return jnp.clip(drawn, -reach, reach).astype(held_as)


def setup_inputs(seed: int = 0) -> dict:
    arg_keys = jax.random.split(jax.random.key(seed), 7)
    return {
        "t2_ph": normal_values(arg_keys[0], (N_CHAN, P_SIZE, H), 1.0, 6.0, ((0, 96), (1, 8))),
        "dest_owner": draw_dest_owner(jax.random.fold_in(arg_keys[6], 71), 0),
        "source_owner": draw_source_owner(jax.random.fold_in(arg_keys[6], 71), 0),
        "source_slot": draw_source_slot(jax.random.fold_in(arg_keys[6], 71), 0),
        "hole_count": draw_hole_count(jax.random.fold_in(arg_keys[6], 71), 0),
        "ladder_v": draw_ladder_v(jax.random.fold_in(arg_keys[6], 71), 0),
    }


def reference(t2_ph, dest_owner, source_owner, source_slot, hole_count, ladder_v):
    owners = dest_owner.reshape(N_CHAN, N_KRED, SLAB)
    channels = jnp.arange(N_CHAN, dtype=jnp.int32)
    matches = (owners[..., None] == channels[None, None, None, :]).astype(jnp.int32)
    before = jnp.sum((jnp.cumsum(matches, axis=2) - matches) * matches, axis=3)
    target = owners * RECV_CAP + before
    row_ids = jnp.broadcast_to(jnp.arange(SLAB, dtype=jnp.int32)[None, None, :], owners.shape)
    sender_ids = jnp.broadcast_to(channels[:, None, None], owners.shape)
    lane_ids = jnp.broadcast_to(jnp.arange(N_KRED, dtype=jnp.int32)[None, :, None], owners.shape)
    table = jnp.zeros((N_CHAN, N_KRED, N_CHAN * RECV_CAP), jnp.int32)
    table = table.at[sender_ids, lane_ids, target].set(row_ids)
    senders = source_owner.reshape(N_CHAN, N_KRED, SLAB)
    slots = source_slot.reshape(N_CHAN, N_KRED, SLAB)
    receivers = sender_ids
    chosen = table[senders, lane_ids, receivers * RECV_CAP + slots]
    recoupled = t2_ph[senders, lane_ids * SLAB + chosen].reshape(N_CHAN, P_SIZE, H)

    def one_channel(operands):
        interaction, amplitudes = operands
        return jnp.dot(interaction, amplitudes, preferred_element_type=jnp.float32)

    ladder = lax.map(one_channel, (ladder_v, recoupled))
    columns = jnp.arange(H, dtype=jnp.int32)
    masked = jnp.where(columns[None, None, :] < hole_count[:, None, None], ladder, jnp.float32(0.0))
    return masked.astype(jnp.bfloat16)
```

```python
import jax
import jax.numpy as jnp
from jax import lax
from jax.sharding import PartitionSpec as P


def on_device(t2_ph, dest_owner, source_owner, source_slot, hole_count, ladder_v):
    ph_rows = t2_ph[0]
    owners = dest_owner[0]
    owners_count = lax.axis_size("chan")
    slabs = lax.axis_size("kred")
    slab_rows, hole_width = ph_rows.shape
    capacity = 2 * slab_rows // owners_count
    matches = (owners[:, None] == jnp.arange(owners_count, dtype=jnp.int32)[None, :]).astype(
        jnp.int32
    )
    before = jnp.sum((jnp.cumsum(matches, axis=0) - matches) * matches, axis=1)
    target = owners * capacity + before
    outbox = jnp.zeros((owners_count * capacity, hole_width), ph_rows.dtype).at[target].set(ph_rows)
    arrived = lax.all_to_all(
        outbox.reshape(owners_count, capacity, hole_width),
        "chan",
        split_axis=0,
        concat_axis=0,
        tiled=True,
    )
    picked = source_owner[0] * capacity + source_slot[0]
    recoupled = arrived.reshape(owners_count * capacity, hole_width)[picked]
    channel = lax.all_to_all(
        jnp.broadcast_to(recoupled[None], (slabs, slab_rows, hole_width)),
        "kred",
        split_axis=0,
        concat_axis=0,
        tiled=True,
    ).reshape(slabs * slab_rows, hole_width)
    ladder = lax.dot_general(
        ladder_v[0],
        channel,
        (((0,), (0,)), ((), ())),
        preferred_element_type=jnp.float32,
    )
    columns = jnp.arange(hole_width, dtype=jnp.int32)
    masked = jnp.where(columns[None, :] < hole_count[0], ladder, jnp.float32(0.0))
    return masked.astype(jnp.bfloat16)[None]


def solution(mesh):
    placed = (
        P("chan", "kred", None),
        P("chan", "kred"),
        P("chan", "kred"),
        P("chan", "kred"),
        P("chan"),
        P("chan", None, "kred"),
    )
    return jax.shard_map(
        on_device, mesh=mesh, in_specs=placed, out_specs=P("chan", "kred", None), check_vma=False
    )
```

```python
import functools

import jax
import jax.numpy as jnp
from jax import lax
from jax.experimental import pallas as pl
from jax.experimental.pallas import tpu as pltpu
from jax.sharding import PartitionSpec as P

BF16, F32 = jnp.bfloat16, jnp.float32
SMALL = pltpu.CompilerParams(vmem_limit_bytes=16 * 2**20)
BOTH_FIRST = (((0,), (0,)), ((), ()))


def one_hot(mask):
    return jnp.where(mask, 1.0, 0.0).astype(BF16)


def pack_rows(owners_count, capacity, owner_ref, rows_ref, outbox_ref):
    rows = rows_ref.shape[0]
    owner = owner_ref[...]
    match = owner == lax.broadcasted_iota(jnp.int32, (owners_count, rows), 0)
    row_at = lax.broadcasted_iota(jnp.int32, (rows, rows), 0)
    earlier = row_at < lax.broadcasted_iota(jnp.int32, (rows, rows), 1)
    counts = jnp.dot(one_hot(match), one_hot(earlier), preferred_element_type=F32)
    before = jnp.sum(jnp.where(match, counts, 0.0), axis=0, keepdims=True)
    target = owner * capacity + before.astype(jnp.int32)
    slots = lax.broadcasted_iota(jnp.int32, (owners_count * capacity, rows), 0)
    outbox_ref[...] = jnp.dot(
        one_hot(slots == target), rows_ref[...], preferred_element_type=F32
    ).astype(BF16)


def pick_rows(capacity, owner_ref, slot_ref, arrived_ref, copies_ref):
    picked = owner_ref[...] * capacity + slot_ref[...]
    slots = lax.broadcasted_iota(jnp.int32, (arrived_ref.shape[0], picked.shape[1]), 0)
    taken = lax.dot_general(
        arrived_ref[...], one_hot(slots == picked), BOTH_FIRST, preferred_element_type=F32
    ).astype(BF16)
    for k in range(copies_ref.shape[0]):
        copies_ref[k] = taken


def contract(hole_ref, channel_ref, weights_ref, out_ref):
    slabs, width, depth = channel_ref.shape
    total = jnp.dot(channel_ref[0], weights_ref[:depth, :], preferred_element_type=F32)
    for k in range(1, slabs):
        total += jnp.dot(
            channel_ref[k],
            weights_ref[k * depth : (k + 1) * depth, :],
            preferred_element_type=F32,
        )
    live = lax.broadcasted_iota(jnp.int32, total.shape, 0) < hole_ref[0]
    out_ref[...] = jnp.where(live, total, 0.0).T.astype(BF16)


def on_device(t2_ph, dest_owner, source_owner, source_slot, hole_count, ladder_v):
    owners_count, slabs = lax.axis_size("chan"), lax.axis_size("kred")
    _, slab_rows, width = t2_ph.shape
    capacity = 2 * slab_rows // owners_count
    slots = owners_count * capacity
    whole = pl.BlockSpec(memory_space=pltpu.VMEM)
    outbox = pl.pallas_call(
        functools.partial(pack_rows, owners_count, capacity),
        out_shape=jax.ShapeDtypeStruct((slots, width), BF16),
        in_specs=[whole] * 2,
        out_specs=whole,
        compiler_params=SMALL,
        name="pack_rows",
    )(dest_owner, t2_ph[0])
    arrived = lax.all_to_all(
        outbox.reshape(owners_count, capacity // 2, 2, width), "chan", 0, 0, tiled=True
    ).reshape(slots, width)
    copies = pl.pallas_call(
        functools.partial(pick_rows, capacity),
        out_shape=jax.ShapeDtypeStruct((slabs, width, slab_rows), BF16),
        in_specs=[whole] * 3,
        out_specs=whole,
        compiler_params=SMALL,
        name="pick_rows",
    )(source_owner, source_slot, arrived)
    channel = lax.all_to_all(copies, "kred", 0, 0, tiled=True)
    ladder = pl.pallas_call(
        contract,
        out_shape=jax.ShapeDtypeStruct((slab_rows, width), BF16),
        in_specs=[pl.BlockSpec(memory_space=pltpu.SMEM), whole, whole],
        out_specs=whole,
        compiler_params=SMALL,
        name="contract",
    )(hole_count, channel, ladder_v[0])
    return ladder[None]


def solution(mesh):
    placed = (
        P("chan", "kred", None),
        P("chan", "kred"),
        P("chan", "kred"),
        P("chan", "kred"),
        P("chan"),
        P("chan", None, "kred"),
    )
    return jax.shard_map(
        on_device, mesh=mesh, in_specs=placed, out_specs=P("chan", "kred", None), check_vma=False
    )
```
